256 devices in a mesh: dp: 16 (over y, z_hi), seq: 16 (over z_lo, x, core).
Axes of the slice: x: 4, y: 4, z: 8 (z_hi: 4, z_lo: 2; z = z_hi * 2 + z_lo), core: 2. Of those that a mesh axis runs over, the one named last changes fastest.
Arguments:
- query: bfloat16 [16, 4096, 2048], P('dp', 'seq'), may hold values from -110 to 110
- key_codes: int32 [16, 4096, 1024], P('dp', 'seq'), may hold values from -127 to 127
- value_codes: int32 [16, 4096, 1024], P('dp', 'seq'), may hold values from -127 to 127
- key_scale: float32 [8], replicated, may hold values from 0.007 to 0.03
- value_scale: float32 [8], replicated, may hold values from 0.007 to 0.03
- out_grad: bfloat16 [16, 4096, 2048], P('dp', 'seq'), may hold values from -60 to 60
- doc_ids: int32 [16, 4096], P('dp', 'seq'), may hold values from 0 to 7, never falling along the last dimension, each value on 1 to 2048 neighbouring positions
Outputs:
- query_grad: bfloat16 [16, 4096, 2048], P('dp', 'seq')
- key_grad: bfloat16 [16, 4096, 1024], P('dp', 'seq')
- value_grad: bfloat16 [16, 4096, 1024], P('dp', 'seq')
- scale_grads: float32 [2, 8], replicated
The draws below stay inside these ranges and needn't reach their ends.
Inputs may be any that keep to these rules, and one draw needn't show every extreme that they name: `doc_ids`: never falling along a sequence.
All inputs are finite; a program needn't handle non-finite values.
Results may differ from the reference program's by a relative error of at most 0.0085.
Values may be sent and summed in bfloat16 or wider, within the bound.
No kernel may reach another device: no remote copies, remote signals or barrier semaphores. Data moves between devices by JAX's collectives and lax.ppermute only.
A program may use at most 128 MiB of HBM per device.

```python
import math
import jax
import jax.numpy as jnp
import numpy as np
from jax import lax

HQ = 16
HK = 8
HD = 128
WINDOW = 1024
TOK_DEV = 256
BATCH = 16
SEQ_LEN = 4096


def code_table(key, salt):
    return jax.random.randint(jax.random.fold_in(key, salt), (BATCH, SEQ_LEN, HK * HD), -127, 128).astype(jnp.int32)


def draw_key_codes(key, part):
    return code_table(key, 11)


def draw_value_codes(key, part):
    return code_table(key, 12)


def draw_query(key, part):
    shape = (BATCH, SEQ_LEN, HQ * HD)
    base = jnp.clip(jax.random.normal(jax.random.fold_in(key, 21), shape, jnp.float32), -6.0, 6.0)
    return base.astype(jnp.bfloat16)


def draw_out_grad(key, part):
    shape = (BATCH, SEQ_LEN, HQ * HD)
    along = jnp.arange(SEQ_LEN, dtype=jnp.float32) / SEQ_LEN
    across = jnp.arange(BATCH, dtype=jnp.float32) / BATCH
    rise = jnp.exp(jnp.log(3.0) * (along[None, :, None] + across[:, None, None]))
    base = jnp.clip(jax.random.normal(jax.random.fold_in(key, 31), shape, jnp.float32), -6.0, 6.0)
    return (base * rise).astype(jnp.bfloat16)


def profile(count, total, limit, skew):
    weights = [(1 << 20) // math.isqrt(standing ** skew) + 1 for standing in range(2, count + 1)]
    rest, counts = total - limit - (count - 1), [1] * (count - 1)
    while rest > 0:
        movable = [i for i in range(count - 1) if counts[i] < limit]
        pool, budget = sum([weights[i] for i in movable]), rest
        for i in movable:
            more = min(limit - counts[i], max(1, budget * weights[i] // pool), rest)
            counts[i] = counts[i] + more
            rest = rest - more
    return np.array([limit] + counts)


def ragged_sizes(stream_key, number_of, total, most, skew):
    if number_of == 2:
        one = jax.random.randint(stream_key, (), max(1, total - most), min(most, total - 1) + 1)
        return jnp.stack([one, total - one])
    tallies = jnp.asarray(profile(number_of, total, most, skew), jnp.int32)
    couples = (number_of - 1) // 2
    source_of, sink = tallies[1:1 + 2 * couples:2], tallies[2:2 + 2 * couples:2]
    room = jnp.minimum(source_of - 1, most - sink)
    moved = jax.random.randint(jax.random.fold_in(stream_key, 1), (couples,), 0, 1 << 20) % (room + 1)
    tallies = tallies.at[1:1 + 2 * couples:2].set(source_of - moved).at[2:2 + 2 * couples:2].set(sink + moved)
    return tallies[jax.random.permutation(jax.random.fold_in(stream_key, 2), number_of)]


def setup_inputs(seed: int = 0) -> dict:
    splits = jax.random.split(jax.random.key(seed), 8)
    query = draw_query(jax.random.fold_in(splits[7], 71), 0)
    key_codes = draw_key_codes(jax.random.fold_in(splits[7], 71), 0)
    value_codes = draw_value_codes(jax.random.fold_in(splits[7], 71), 0)
    key_scale = jnp.clip(jnp.exp(jax.random.uniform(splits[3], (HK,), jnp.float32, math.log(0.007), math.log(0.03))), 0.007, 0.03)
    value_scale = jnp.clip(jnp.exp(jax.random.uniform(splits[4], (HK,), jnp.float32, math.log(0.007), math.log(0.03))), 0.007, 0.03)
    out_grad = draw_out_grad(jax.random.fold_in(splits[7], 71), 0)
    doc_ids = jax.vmap(lambda own: jnp.searchsorted(jnp.cumsum(ragged_sizes(own, SEQ_LEN // (2 * TOK_DEV), SEQ_LEN, min(2 * WINDOW, 3 * SEQ_LEN // 4), 2)), jnp.arange(SEQ_LEN), side="right"))(jax.random.split(splits[6], BATCH)).reshape((BATCH, SEQ_LEN)).astype(jnp.int32)
    return {"query": query, "key_codes": key_codes, "value_codes": value_codes, "key_scale": key_scale, "value_scale": value_scale, "out_grad": out_grad, "doc_ids": doc_ids}


attn_scale = 168.0 ** -0.5


def head_grads(q_rows, keys, values, grad_rows, q_doc, k_doc, q_pos, k_pos):
    rows = q_rows.shape[0]
    span = keys.shape[0]
    group = HQ // HK
    q_heads = q_rows.reshape(rows, HK, group, HD).transpose(1, 2, 0, 3)
    k_heads = keys.reshape(span, HK, HD).transpose(1, 0, 2)
    v_heads = values.reshape(span, HK, HD).transpose(1, 0, 2)
    g_heads = grad_rows.reshape(rows, HK, group, HD).transpose(1, 2, 0, 3)
    allowed = (q_doc[:, None] == k_doc[None, :]) & (k_pos[None, :] <= q_pos[:, None])
    allowed = allowed & (q_pos[:, None] - k_pos[None, :] < WINDOW) & (k_pos[None, :] >= 0)

    def one_head(parts):
        qg, kg, vg, gg = parts
        qf = qg.astype(jnp.float32)
        kf = kg.astype(jnp.float32)
        vf = vg.astype(jnp.float32)
        gf = gg.astype(jnp.float32)
        scores = jnp.einsum("gtd,ld->gtl", qf, kf) * attn_scale
        scores = jnp.where(allowed[None], scores, -jnp.inf)
        top = jnp.max(scores, axis=-1, keepdims=True)
        weights = jnp.exp(scores - top)
        probs = weights / jnp.sum(weights, axis=-1, keepdims=True)
        probs_low = probs.astype(jnp.bfloat16).astype(jnp.float32)
        attended = jnp.einsum("gtl,ld->gtd", probs_low, vf)
        delta = jnp.sum(gf * attended, axis=-1, keepdims=True)
        dprobs = jnp.einsum("gtd,ld->gtl", gf, vf)
        dscores = (probs * (dprobs - delta)).astype(jnp.bfloat16).astype(jnp.float32)
        dq = (jnp.einsum("gtl,ld->gtd", dscores, kf) * attn_scale).astype(jnp.bfloat16)
        dk = jnp.einsum("gtl,gtd->ld", dscores, qf) * attn_scale
        dv = jnp.einsum("gtl,gtd->ld", probs_low, gf)
        return dq, dk, dv

    dq, dk, dv = lax.map(one_head, (q_heads, k_heads, v_heads, g_heads))
    dq = dq.transpose(2, 0, 1, 3).reshape(rows, HQ * HD)
    dk = dk.transpose(1, 0, 2).reshape(span, HK * HD)
    dv = dv.transpose(1, 0, 2).reshape(span, HK * HD)
    return dq, dk, dv


def dequantize(codes, scale):
    rows = codes.shape[0]
    full = codes.reshape(rows, HK, HD).astype(jnp.float32) * scale[None, :, None]
    return full.reshape(rows, HK * HD).astype(jnp.bfloat16)


def assemble(parts, reach, nblk):
    total = parts[:, reach]
    for back in range(1, reach + 1):
        piece = lax.optimization_barrier(parts[back:, reach - back].astype(jnp.bfloat16)).astype(jnp.float32)
        filler = jnp.zeros((back,) + piece.shape[1:], jnp.float32)
        total = total + jnp.concatenate([piece, filler], axis=0)
    return total.reshape(nblk * TOK_DEV, HK * HD)


def reference(query, key_codes, value_codes, key_scale, value_scale, out_grad, doc_ids):
    nblk = SEQ_LEN // TOK_DEV
    reach = WINDOW // TOK_DEV
    pad = reach * TOK_DEV
    span = pad + TOK_DEV

    def one_seq(parts):
        q, kc, vc, g, doc = parts
        keys = dequantize(kc, key_scale)
        values = dequantize(vc, value_scale)
        keys_p = jnp.concatenate([jnp.zeros((pad, HK * HD), jnp.bfloat16), keys], axis=0)
        values_p = jnp.concatenate([jnp.zeros((pad, HK * HD), jnp.bfloat16), values], axis=0)
        doc_p = jnp.concatenate([jnp.zeros((pad,), jnp.int32), doc], axis=0)

        def block(c):
            start = (c * TOK_DEV).astype(jnp.int32)
            qb = lax.dynamic_slice_in_dim(q, start, TOK_DEV, 0)
            gb = lax.dynamic_slice_in_dim(g, start, TOK_DEV, 0)
            qd = lax.dynamic_slice_in_dim(doc, start, TOK_DEV, 0)
            kb = lax.dynamic_slice_in_dim(keys_p, start, span, 0)
            vb = lax.dynamic_slice_in_dim(values_p, start, span, 0)
            kd = lax.dynamic_slice_in_dim(doc_p, start, span, 0)
            q_pos = start + jnp.arange(TOK_DEV, dtype=jnp.int32)
            k_pos = start - pad + jnp.arange(span, dtype=jnp.int32)
            dq, dk, dv = head_grads(qb, kb, vb, gb, qd, kd, q_pos, k_pos)
            return dq, dk.reshape(reach + 1, TOK_DEV, HK * HD), dv.reshape(reach + 1, TOK_DEV, HK * HD)

        dq, dk, dv = lax.map(block, jnp.arange(nblk, dtype=jnp.int32))
        key_total = assemble(dk, reach, nblk)
        value_total = assemble(dv, reach, nblk)
        ks = jnp.sum((key_total * kc.astype(jnp.float32)).reshape(SEQ_LEN, HK, HD), axis=(0, 2))
        vs = jnp.sum((value_total * vc.astype(jnp.float32)).reshape(SEQ_LEN, HK, HD), axis=(0, 2))
        return (dq.reshape(SEQ_LEN, HQ * HD), key_total.astype(jnp.bfloat16),
                value_total.astype(jnp.bfloat16), jnp.stack([ks, vs]))

    dq, dk, dv, sums = lax.map(one_seq, (query, key_codes, value_codes, out_grad, doc_ids))
    scale_grads = jnp.sum(sums, axis=0) / (BATCH * SEQ_LEN)
    return (dq, dk, dv, scale_grads)
```

```python
import jax
import jax.numpy as jnp
from jax import lax
from jax.experimental import pallas as pl
from jax.experimental.pallas import tpu as pltpu
from jax.sharding import PartitionSpec as P

HQ = 16
HK = 8
HD = 128
WINDOW = 1024
TOK = 256
HALF = HK // 2
DOCS = 8
NEG = -1e30

attn_scale = 168.0 ** (-0.5)
exp_scale = attn_scale * 1.4426950408889634

bf16 = jnp.bfloat16
f32 = jnp.float32
KV = 2 * HD
DOC_ROWS = 16


def pack_kernel(meta, kc, vc, doc, out):
    row = lax.broadcasted_iota(jnp.int32, (DOC_ROWS, TOK), 0)
    docs = jnp.broadcast_to(doc[...].astype(f32), (DOC_ROWS, TOK))
    out[HALF * TOK :, :] = jnp.where(row == 0, docs, 0.0).astype(bf16)
    for j in range(HALF):
        rows = slice(j * TOK, (j + 1) * TOK)
        cols = slice(j * HD, (j + 1) * HD)
        out[rows, :HD] = kc[:, cols].astype(f32).astype(bf16)
        out[rows, HD:] = vc[:, cols].astype(f32).astype(bf16)


def pack(meta, kc, vc, doc, other):
    half = lambda i, m: (0, 1 - m[0] if other else m[0])
    rows = HALF * TOK + DOC_ROWS
    return pl.pallas_call(
        pack_kernel,
        grid_spec=pltpu.PrefetchScalarGridSpec(
            num_scalar_prefetch=1,
            grid=(1,),
            in_specs=[
                pl.BlockSpec((TOK, HALF * HD), half),
                pl.BlockSpec((TOK, HALF * HD), half),
                pl.BlockSpec((1, TOK), lambda i, m: (0, 0)),
            ],
            out_specs=pl.BlockSpec((rows, KV), lambda i, m: (0, 0)),
        ),
        out_shape=jax.ShapeDtypeStruct((rows, KV), bf16),
        compiler_params=pltpu.CompilerParams(vmem_limit_bytes=16 << 20),
        cost_estimate=pl.CostEstimate(flops=1 << 19, bytes_accessed=3 << 19, transcendentals=0),
        name="pack",
    )(meta, kc, vc, doc)


def rows_kernel(meta, q, g, out):
    width = HQ // 2 * HD
    out[:, :width] = q[...]
    out[:, width:] = g[...]


def pack_rows(meta, q, g):
    width = HQ // 2 * HD
    other = lambda i, m: (0, 1 - m[0])
    return pl.pallas_call(
        rows_kernel,
        grid_spec=pltpu.PrefetchScalarGridSpec(
            num_scalar_prefetch=1,
            grid=(1,),
            in_specs=[pl.BlockSpec((TOK, width), other)] * 2,
            out_specs=pl.BlockSpec((TOK, 2 * width), lambda i, m: (0, 0)),
        ),
        out_shape=jax.ShapeDtypeStruct((TOK, 2 * width), bf16),
        compiler_params=pltpu.CompilerParams(vmem_limit_bytes=16 << 20),
        cost_estimate=pl.CostEstimate(flops=1 << 19, bytes_accessed=2 << 20, transcendentals=0),
        name="pack_rows",
    )(meta, q, g)


def combine_kernel(own, came, *outs):
    docs = slice(HALF * TOK, HALF * TOK + DOC_ROWS)
    for slot, src in enumerate((own, came)):
        outs[0][slot, TOK:, :] = src[docs, :]
        for j in range(HALF):
            outs[j][slot, :TOK, :] = src[j * TOK : (j + 1) * TOK, :]


def combine(own, came):
    shapes = [(2, TOK + (DOC_ROWS if j == 0 else 0), KV) for j in range(HALF)]
    return pl.pallas_call(
        combine_kernel,
        out_shape=[jax.ShapeDtypeStruct(s, bf16) for s in shapes],
        compiler_params=pltpu.CompilerParams(vmem_limit_bytes=16 << 20),
        cost_estimate=pl.CostEstimate(flops=1 << 19, bytes_accessed=2 << 20, transcendentals=0),
        name="combine",
    )(own, came)


def dot_nt(a, b):
    return lax.dot_general(a, b, (((1,), (1,)), ((), ())), preferred_element_type=f32)


def dot_nn(a, b):
    return lax.dot_general(a, b, (((1,), (0,)), ((), ())), preferred_element_type=f32)


def attn_kernel(j, meta, kscale, vscale, qo, qr, go, gr, blk_a, blk_n, blk_f, doc_a, doc_n, doc_f,
                dq, grad_f, grad_n, grad_a, terms, kk, vv, kt, ss, dp, pp, ds):
    core = meta[0]
    chip = meta[1]
    ks = kscale[core * HALF + j]
    vs = vscale[core * HALF + j]
    parts = (blk_f, blk_n, blk_a)
    grads = (grad_f, grad_n, grad_a)
    docs = (doc_f, doc_n, doc_a)

    rows = []
    for kb in range(6):
        row = docs[kb // 2][(kb % 2) ^ core, 0:1, :].astype(f32)
        if kb < 4:
            row = jnp.where(chip < (2 if kb < 2 else 1), -1.0, row)
        rows.append(row)
    lows = []
    for t in range(2):
        lane = lax.broadcasted_iota(jnp.int32, (1, TOK), 1).astype(f32)
        lows.append(lane + float(t * TOK + 1))
    begin = [jnp.zeros((1, TOK), f32), jnp.zeros((1, TOK), f32)]
    for v in range(DOCS):
        less = sum(jnp.where(r < v, 1.0, 0.0) for r in rows)
        count = jnp.sum(less, axis=1, keepdims=True)
        for t in range(2):
            begin[t] = jnp.where(rows[4 + t] == v, count, begin[t])
    lows = [jnp.maximum(a, b) for a, b in zip(lows, begin)]

    for kb in range(6):
        src = parts[kb // 2]
        slot = (kb % 2) ^ core
        at = slice(kb * TOK, (kb + 1) * TOK)
        k = (src[slot, :TOK, :HD].astype(f32) * ks).astype(bf16)
        kk[at, :] = k
        kt[:, at] = k.T
        vv[at, :] = (src[slot, :TOK, HD:].astype(f32) * vs).astype(bf16)

    sub = lax.broadcasted_iota(jnp.int32, (TOK, TOK), 0).astype(f32)
    lane = lax.broadcasted_iota(jnp.int32, (TOK, TOK), 1).astype(f32)
    qs, gs = [], []
    for t in range(2):
        q = jnp.where(core == t, qo[...], qr[...])
        g = jnp.where(core == t, go[...], gr[...])
        qs.append(jnp.concatenate([q[:, :HD], q[:, HD:]], axis=0))
        gs.append(jnp.concatenate([g[:, :HD], g[:, HD:]], axis=0))

    for t in range(2):
        q, g, low = qs[t], gs[t], lows[t]
        top = None
        for n in range(5):
            kb = t + n
            at = slice(kb * TOK, (kb + 1) * TOK)
            here = slice(n * TOK, (n + 1) * TOK)
            s = dot_nt(kk[at, :], q)
            seen = sub >= low - float(kb * TOK)
            if n == 4:
                seen = seen & (sub <= lane)
            s0 = jnp.where(seen, s[:, :TOK], NEG)
            s1 = jnp.where(seen, s[:, TOK:], NEG)
            ss[here, :TOK] = s0
            ss[here, TOK:] = s1
            m = jnp.concatenate([jnp.max(s0, axis=0, keepdims=True), jnp.max(s1, axis=0, keepdims=True)], axis=1)
            top = m if top is None else jnp.maximum(top, m)
        norm = None
        for n in range(5):
            here = slice(n * TOK, (n + 1) * TOK)
            e = jnp.exp2((ss[here, :] - top) * exp_scale)
            ss[here, :] = e
            l = jnp.sum(e, axis=0, keepdims=True)
            norm = l if norm is None else norm + l
        inv = 1.0 / norm
        delta = None
        for n in range(5):
            kb = t + n
            at = slice(kb * TOK, (kb + 1) * TOK)
            here = slice(n * TOK, (n + 1) * TOK)
            d = dot_nt(vv[at, :], g)
            low_p = (ss[here, :] * inv).astype(bf16)
            pp[t, here, :] = low_p
            dp[here, :] = d
            part = jnp.sum(low_p.astype(f32) * d, axis=0, keepdims=True)
            delta = part if delta is None else delta + part
        for n in range(5):
            here = slice(n * TOK, (n + 1) * TOK)
            ds[t, here, :] = ((ss[here, :] * inv) * (dp[here, :] - delta)).astype(bf16)
        got = dot_nn(kt[:, t * TOK : (t + 5) * TOK], ds[t]) * attn_scale
        slot = t ^ core
        dq[slot, :, :HD] = got[:, :TOK].T.astype(bf16)
        dq[slot, :, HD:] = got[:, TOK:].T.astype(bf16)

    k_terms = jnp.zeros((1, HD), f32)
    v_terms = jnp.zeros((1, HD), f32)
    for kb in range(6):
        dk = dv = None
        for t in range(2):
            n = kb - t
            if 0 <= n < 5:
                here = slice(n * TOK, (n + 1) * TOK)
                a = dot_nn(ds[t, here, :], qs[t])
                b = dot_nn(pp[t, here, :], gs[t])
                dk = a if dk is None else dk + a
                dv = b if dv is None else dv + b
        dk = dk * attn_scale
        slot = (kb % 2) ^ core
        src, out = parts[kb // 2], grads[kb // 2]
        k_terms = k_terms + jnp.sum(dk * src[slot, :TOK, :HD].astype(f32), axis=0, keepdims=True)
        v_terms = v_terms + jnp.sum(dv * src[slot, :TOK, HD:].astype(f32), axis=0, keepdims=True)
        out[slot, :, :HD] = dk.astype(out.dtype)
        out[slot, :, HD:] = dv.astype(out.dtype)
    row = lax.broadcasted_iota(jnp.int32, (8, HD), 0)
    terms[...] = jnp.where(row == 0, k_terms, jnp.where(row == 1, v_terms, 0.0))


def attend(j, meta, kscale, vscale, q, g, came, blk_a, blk_n, blk_f, doc_a, doc_n, doc_f):
    own = lambda i, m: (0, m[0] * HALF + j)
    block = pl.BlockSpec((2, TOK, KV), lambda i, m: (0, 0, 0))
    doc = pl.BlockSpec((2, DOC_ROWS, KV), lambda i, m: (0, TOK // DOC_ROWS, 0))
    scale = pl.BlockSpec(memory_space=pltpu.SMEM)
    pair = 2 * HD
    shape = lambda d: jax.ShapeDtypeStruct((2, TOK, KV), d)
    return pl.pallas_call(
        lambda *refs: attn_kernel(j, *refs),
        grid_spec=pltpu.PrefetchScalarGridSpec(
            num_scalar_prefetch=1,
            grid=(1,),
            in_specs=[
                scale,
                scale,
                pl.BlockSpec((TOK, pair), own),
                pl.BlockSpec((TOK, pair), lambda i, m: (0, j)),
                pl.BlockSpec((TOK, pair), own),
                pl.BlockSpec((TOK, pair), lambda i, m: (0, HALF + j)),
                block,
                block,
                block,
                doc,
                doc,
                doc,
            ],
            out_specs=[block, block, block, block, pl.BlockSpec((8, HD), lambda i, m: (0, 0))],
            scratch_shapes=[
                pltpu.VMEM((6 * TOK, HD), bf16),
                pltpu.VMEM((6 * TOK, HD), bf16),
                pltpu.VMEM((HD, 6 * TOK), bf16),
                pltpu.VMEM((5 * TOK, 2 * TOK), f32),
                pltpu.VMEM((5 * TOK, 2 * TOK), f32),
                pltpu.VMEM((2, 5 * TOK, 2 * TOK), bf16),
                pltpu.VMEM((2, 5 * TOK, 2 * TOK), bf16),
            ],
        ),
        out_shape=[shape(bf16), shape(bf16), shape(f32), shape(f32), jax.ShapeDtypeStruct((8, HD), f32)],
        compiler_params=pltpu.CompilerParams(vmem_limit_bytes=32 << 20),
        cost_estimate=pl.CostEstimate(flops=2_000_000_000, bytes_accessed=4 << 20, transcendentals=1 << 20),
        name=f"attend{j}",
    )(meta, kscale, vscale, q, came, g, came, blk_a, blk_n, blk_f, doc_a, doc_n, doc_f)


def finish_kernel(meta, *refs):
    own_q, came_q = refs[0:HALF], refs[HALF]
    own_t, came_t = refs[HALF + 1 : 2 * HALF + 1], refs[2 * HALF + 1]
    dq, dk, dv = refs[2 * HALF + 2 :]
    i = pl.program_id(0)

    @pl.when(i == 0)
    def _():
        for j in range(HALF):
            dq[:, j * KV : (j + 1) * KV] = own_q[j][0]
            dk[:, j * HD : (j + 1) * HD] = own_t[j][0, :, :HD]
            dv[:, j * HD : (j + 1) * HD] = own_t[j][0, :, HD:]

    @pl.when(i == 1)
    def _():
        for j in range(HALF):
            dq[:, j * KV : (j + 1) * KV] = came_q[j]
            dk[:, j * HD : (j + 1) * HD] = came_t[j, :, :HD]
            dv[:, j * HD : (j + 1) * HD] = came_t[j, :, HD:]


def finish(meta, own_q, came_q, own_t, came_t):
    first = pl.BlockSpec((1, TOK, KV), lambda i, m: (0, 0, 0))
    whole = pl.BlockSpec((HALF, TOK, KV), lambda i, m: (0, 0, 0))
    place = lambda i, m: (0, i ^ m[0])
    return pl.pallas_call(
        finish_kernel,
        grid_spec=pltpu.PrefetchScalarGridSpec(
            num_scalar_prefetch=1,
            grid=(2,),
            in_specs=[first] * HALF + [whole] + [first] * HALF + [whole],
            out_specs=[
                pl.BlockSpec((TOK, HALF * KV), place),
                pl.BlockSpec((TOK, HALF * HD), place),
                pl.BlockSpec((TOK, HALF * HD), place),
            ],
        ),
        out_shape=[
            jax.ShapeDtypeStruct((TOK, HQ * HD), bf16),
            jax.ShapeDtypeStruct((TOK, HK * HD), bf16),
            jax.ShapeDtypeStruct((TOK, HK * HD), bf16),
        ],
        compiler_params=pltpu.CompilerParams(vmem_limit_bytes=16 << 20),
        cost_estimate=pl.CostEstimate(flops=1 << 19, bytes_accessed=4 << 20, transcendentals=0),
        name="finish",
    )(meta, *own_q, came_q, *own_t, came_t)


def local(query, key_codes, value_codes, key_scale, value_scale, out_grad, doc_ids):
    size = lax.axis_size("seq")
    place = lax.axis_index("seq")
    meta = jnp.stack([place % 2, place // 2]).astype(jnp.int32)
    swap = [(i, i ^ 1) for i in range(size)]
    ahead = [(i, (i + 2) % size) for i in range(size)]
    behind = [(i, (i - 2) % size) for i in range(size)]
    q, g = query[0], out_grad[0]

    send = pack(meta, key_codes[0], value_codes[0], doc_ids, True)
    came = lax.ppermute(send, "seq", swap)
    own = pack(meta, key_codes[0], value_codes[0], doc_ids, False)
    rows = lax.ppermute(pack_rows(meta, q, g), "seq", swap)
    blk_a = combine(own, came)
    blk_n = [lax.ppermute(b, "seq", ahead) for b in blk_a]
    blk_f = [lax.ppermute(b, "seq", ahead) for b in blk_n]

    dqs, totals, terms = [], [], []
    for j in range(HALF):
        dq, part_f, part_n, part_a, term = attend(
            j, meta, key_scale, value_scale, q, g, rows, blk_a[j], blk_n[j], blk_f[j], blk_a[0], blk_n[0], blk_f[0]
        )
        came_f = lax.ppermute(part_f, "seq", behind)
        sent = (part_n + came_f.astype(f32)).astype(bf16)
        came_n = lax.ppermute(sent, "seq", behind)
        dqs.append(dq)
        totals.append((part_a + came_n.astype(f32)).astype(bf16))
        terms.append(jnp.sum(term[:2], axis=1))

    came_q = lax.ppermute(jnp.stack([d[1] for d in dqs]), "seq", swap)
    came_t = lax.ppermute(jnp.stack([t[1] for t in totals]), "seq", swap)
    dq, dk, dv = finish(meta, dqs, came_q, totals, came_t)

    mine = jnp.stack(terms, axis=1)
    none = jnp.zeros_like(mine)
    sums = jnp.where(place % 2 == 0, jnp.concatenate([mine, none], axis=1), jnp.concatenate([none, mine], axis=1))
    for axis in ("seq", "dp"):
        step = 1
        while step < lax.axis_size(axis):
            sums = sums + lax.ppermute(sums, axis, [(i, i ^ step) for i in range(lax.axis_size(axis))])
            step *= 2
    tokens = lax.axis_size("dp") * query.shape[0] * size * TOK
    return dq[None], dk[None], dv[None], sums / tokens


def solution(mesh):
    return jax.shard_map(
        local,
        mesh=mesh,
        in_specs=(
            P("dp", "seq", None),
            P("dp", "seq", None),
            P("dp", "seq", None),
            P(),
            P(),
            P("dp", "seq", None),
            P("dp", "seq"),
        ),
        out_specs=(P("dp", "seq", None), P("dp", "seq", None), P("dp", "seq", None), P()),
        check_vma=False,
    )
```
